32 devices in a mesh: section: 2 (over x), expert: 16 (over z, y, core).
Axes of the slice: x: 2, y: 2, z: 4, core: 2. Of those that a mesh axis runs over, the one named last changes fastest.
Arguments:
- tokens: bfloat16 [4, 512, 2048], P(None, 'expert'), may hold values from -6 to 6
- attn_norm: float32 [2, 2048], P('section'), may hold values from 0.5 to 2
- moe_norm: float32 [2, 2048], P('section'), may hold values from 0.5 to 2
- query_weight: bfloat16 [2, 2048, 1024], P('section', 'expert'), may hold values from -4 to 4
- key_weight: bfloat16 [2, 2048, 128], P('section', 'expert'), may hold values from -0.125 to 0.125
- value_weight: bfloat16 [2, 2048, 128], P('section', 'expert'), may hold values from -0.125 to 0.125
- out_weight: bfloat16 [2, 1024, 2048], P('section', 'expert'), may hold values from -0.1875 to 0.1875
- gate_proj: bfloat16 [2, 16, 2048, 704], P('section', 'expert'), may hold values from -0.125 to 0.125
- up_proj: bfloat16 [2, 16, 2048, 704], P('section', 'expert'), may hold values from -0.125 to 0.125
- down_proj: bfloat16 [2, 16, 704, 2048], P('section', 'expert'), may hold values from -0.21875 to 0.21875
- routes: int32 [2, 4, 512, 6], P('section', None, 'expert'), may hold values from 0 to 15, all different within a row; in each aligned block of 32 rows (0 to 31, 32 to 63, ..., all dimensions but the last counted through in order) at most 16 rows name the same one
- weights_code: int32 [2, 4, 512, 6], P('section', None, 'expert'), may hold values from 8 to 64
Outputs:
- hidden_states: bfloat16 [2, 4, 512, 2048], P('section', None, 'expert')
The draws below stay inside these ranges and needn't reach their ends.
Inputs may be any that keep to these rules, and one draw needn't show every extreme that they name: `routes`: each row names 6 different experts. In each aligned block of 32 rows (one sequence's tokens of one micro-batch of one layer) no expert is named by more than 16 rows, a bound that some block reaches.
All inputs are finite; a program needn't handle non-finite values.
Results may differ from the reference program's by a relative error of at most 0.03.
Values may be sent and summed in bfloat16 or wider, within the bound.
A program may use at most 128 MiB of HBM per device.

```python
import math
import jax
import jax.numpy as jnp
import numpy as np
from jax import lax

D = 2048
FF = 704
HEADS = 8
HEAD_WIDTH = 128
TOP = 6
MICRO = 4
TOK_DEV = 32
LAYERS = 2
EXPERTS = 16
SEQ = 128
TOKENS = 512
CAP = 16
N_EXPERT = 16


def attention_draw(key):
    base_key = jax.random.fold_in(key, 31)
    first_key, second_key = jax.random.split(base_key, 2)
    key_part = jax.random.normal(first_key, (LAYERS, D, HEAD_WIDTH), jnp.float32) / jnp.sqrt(jnp.float32(D))
    key_part = jnp.clip(key_part, -0.125, 0.125)
    noise_part = jax.random.normal(second_key, (LAYERS, D, HEADS * HEAD_WIDTH), jnp.float32) / jnp.sqrt(jnp.float32(D))
    query_part = noise_part
    return (jnp.clip(query_part, -4.0, 4.0), key_part)


def draw_query_weight(key, part):
    return attention_draw(key)[0].astype(jnp.bfloat16)


def draw_key_weight(key, part):
    return attention_draw(key)[1].astype(jnp.bfloat16)


def with_ends(result, own_key, least, high):
    place = [jax.random.randint(jax.random.fold_in(own_key, axis), (), 0, length) for axis, length in enumerate(result.shape)]
    longest = result.shape.index(max(result.shape))
    neighbour = place[:longest] + [(place[longest] + 1) % result.shape[longest]] + place[longest + 1:]
    return result.at[tuple(place)].set(least).at[tuple(neighbour)].set(high)


def shard_levels(stream_key, dims, cuts, smallest, top_value):
    level, own = 1.0, jax.random.fold_in(stream_key, 6)
    for dim, parts in cuts:
        draws = jnp.exp(jax.random.uniform(jax.random.fold_in(own, dim), (parts,), jnp.float32, smallest / len(cuts), top_value / len(cuts)))
        level = level * jnp.repeat(draws, dims[dim] // parts).reshape([-1 if axis == dim else 1 for axis in range(len(dims))])
    return level


def deal_out(stream_key, own, number, rows, amount, top, limit, slope):
    ranking = jax.random.permutation(stream_key, amount)
    crowded, usual = shares(amount, rows * top, limit, slope, True), shares(amount, rows * top, limit, slope, False)
    places = jnp.arange(amount)

    def named(lengths, rotation):
        used = int((lengths > 0).sum())
        fixed = max(1, used // 4)
        passed = fixed + (places - fixed + rotation * (used - fixed)) % max(1, amount - fixed)
        return jnp.zeros((amount,), jnp.int32).at[ranking[jnp.where(places < fixed, places, passed)]].set(jnp.asarray(lengths, jnp.int32))

    lengths = jnp.where(number % 4 == 0, named(crowded, number // 4), named(usual, number - number // 4 - 1))
    mixed = jax.random.permutation(jax.random.fold_in(own, 3), amount)
    giver, receiver = mixed[0:amount // 2 * 2:2], mixed[1:amount // 2 * 2:2]
    slack = jnp.minimum(lengths[giver] - 1, limit - lengths[receiver]) // 2
    slack = jnp.where((giver == ranking[0]) | (receiver == ranking[0]) | (lengths[receiver] == 0), 0, jnp.maximum(slack, 0))
    passed = jax.random.randint(jax.random.fold_in(own, 4), (amount // 2,), 0, 1 << 20) % (slack + 1)
    lengths = lengths.at[giver].add(-passed).at[receiver].add(passed)
    members = jnp.searchsorted(jnp.cumsum(lengths), jnp.arange(rows * top), side="right").astype(jnp.int32)
    grid = members.reshape(top, rows).T
    grid = grid[jax.random.permutation(jax.random.fold_in(own, 1), rows)]
    rotation = jax.random.randint(jax.random.fold_in(own, 2), (rows, 1), 0, top)
    return jnp.take_along_axis(grid, (jnp.arange(top)[None, :] + rotation) % top, axis=1)


def shares(number_of, total, reach, lean, full):
    loads = [(1 << 20) // math.isqrt(standing ** lean) + 1 for standing in range(1, number_of + 1)]
    largest = reach if full else min(reach, max(-(-total // number_of), total * loads[0] // sum(loads)))
    least = 1 if total - largest >= number_of - 1 else 0
    given, spare = [largest] + [least] * (number_of - 1), total - largest - least * (number_of - 1)
    while spare > 0:
        candidates = [i for i in range(1, number_of) if given[i] < largest] or [i for i in range(1, number_of) if given[i] < reach]
        mass, left = sum([loads[i] for i in candidates]), spare
        for i in candidates:
            extra = min(reach - given[i], max(1, left * loads[i] // mass), spare)
            given[i] = given[i] + extra
            spare = spare - extra
    return np.array(given)


def noise(rng, dims, width, limit, pieces=(), held_as=jnp.bfloat16):
    factor_of = shard_levels(rng, dims, pieces, -0.22, 0.18) if pieces else 1.0
    values = jax.random.normal(rng, dims, jnp.float32) * width * factor_of
    return jnp.minimum(jnp.maximum(values, -limit), limit).astype(held_as)


def setup_inputs(seed: int = 0) -> dict:
    seeds = jax.random.split(jax.random.key(seed), 13)
    tokens = noise(seeds[0], (MICRO, TOKENS, D), 1.0, 6.0, ((1, 16),))
    attn_norm = jnp.clip(jnp.exp(math.log(2.0) - 1.3862944 * jax.random.uniform(seeds[1], (LAYERS, D), jnp.float32) ** shard_levels(seeds[1], (LAYERS, D), ((0, 2),), -0.2, 0.2)), 0.5, 2.0)
    moe_norm = jnp.clip(jnp.exp(math.log(2.0) - 1.3862944 * jax.random.uniform(seeds[2], (LAYERS, D), jnp.float32) ** shard_levels(seeds[2], (LAYERS, D), ((0, 2),), -0.2, 0.2)), 0.5, 2.0)
    query_weight = draw_query_weight(jax.random.fold_in(seeds[12], 71), 0)
    key_weight = draw_key_weight(jax.random.fold_in(seeds[12], 71), 0)
    value_weight = noise(seeds[5], (LAYERS, D, HEAD_WIDTH), D ** -0.5, 0.125, ((0, 2), (1, 16)))
    out_weight = noise(seeds[6], (LAYERS, HEADS * HEAD_WIDTH, D), (HEADS * HEAD_WIDTH) ** -0.5, 0.1875, ((0, 2), (1, 16)))
    gate_proj = noise(seeds[7], (LAYERS, EXPERTS, D, FF), D ** -0.5, 0.125, ((0, 2), (1, 16)))
    up_proj = noise(seeds[8], (LAYERS, EXPERTS, D, FF), D ** -0.5, 0.125, ((0, 2), (1, 16)))
    down_proj = noise(seeds[9], (LAYERS, EXPERTS, FF, D), FF ** -0.5, 0.21875, ((0, 2), (1, 16)))
    routes_keys = jax.random.split(jax.random.fold_in(seeds[10], 1), LAYERS * MICRO * TOKENS // TOK_DEV)
    routes_turns = jax.random.permutation(jax.random.fold_in(seeds[10], 3), LAYERS * MICRO * TOKENS // TOK_DEV)
    routes = jax.vmap(lambda own, number: deal_out(jax.random.fold_in(seeds[10], 2), own, number, TOK_DEV, EXPERTS, TOP, CAP, 1))(routes_keys, routes_turns).reshape((LAYERS, MICRO, TOKENS, TOP))
    weights_code = with_ends(jax.random.randint(seeds[11], (LAYERS, MICRO, TOKENS, TOP), 8, 65), jax.random.fold_in(seeds[11], 1), 8, 64).astype(jnp.int32)
    return {"tokens": tokens, "attn_norm": attn_norm, "moe_norm": moe_norm, "query_weight": query_weight, "key_weight": key_weight, "value_weight": value_weight, "out_weight": out_weight, "gate_proj": gate_proj, "up_proj": up_proj, "down_proj": down_proj, "routes": routes, "weights_code": weights_code}


epsilon = 1e-06

def rms_scale(features, gain_vector):
    return features * lax.rsqrt(lax.optimization_barrier(jnp.mean(features * features, axis=-1, keepdims=True)) + epsilon) * gain_vector

def expert_rows(slot_rows, gate_matrix, up_matrix, down_matrix):
    gated = jnp.dot(slot_rows, gate_matrix, preferred_element_type=jnp.float32)
    lifted = jnp.dot(slot_rows, up_matrix, preferred_element_type=jnp.float32)
    hidden = (jax.nn.silu(gated) * lifted).astype(jnp.bfloat16)
    return jnp.dot(hidden, down_matrix, preferred_element_type=jnp.float32).astype(jnp.bfloat16)

def apply_expert(expert_item):
    return expert_rows(expert_item[0], expert_item[1], expert_item[2], expert_item[3])

def mixture(normed, picks, codes, gate_all, up_all, down_all):
    assigned = picks.reshape(-1).astype(jnp.int32)
    assigned_count = assigned.shape[0]
    ordering = jnp.argsort(assigned, stable=True).astype(jnp.int32)
    sorted_ids = assigned[ordering]
    counts = lax.optimization_barrier(jnp.sum((assigned[:, None] == jnp.arange(EXPERTS, dtype=jnp.int32)[None, :]).astype(jnp.int32), axis=0))
    starts = jnp.cumsum(counts).astype(jnp.int32) - counts
    bound_rows = CAP * N_EXPERT
    slot_ranks = jnp.arange(assigned_count, dtype=jnp.int32) - starts[sorted_ids]
    places = sorted_ids * bound_rows + slot_ranks
    source_rows = normed[ordering // TOP]
    buffer = jnp.zeros((EXPERTS * bound_rows, D), normed.dtype).at[places].set(source_rows)
    buffer = buffer.reshape(EXPERTS, bound_rows, D)
    outputs = lax.map(apply_expert, (buffer, gate_all, up_all, down_all))
    results = outputs.reshape(EXPERTS * bound_rows, D)[places]
    unsorted = jnp.zeros_like(results).at[ordering].set(results)
    pick_weights = codes.astype(jnp.float32) / 64.0
    return lax.optimization_barrier(jnp.sum(unsorted.astype(jnp.float32).reshape(-1, TOP, D) * pick_weights[:, :, None], axis=1))

def attention(sequences, gain_vector, query_matrix, key_matrix, value_matrix, out_matrix):
    normed = rms_scale(sequences.astype(jnp.float32), gain_vector).astype(jnp.bfloat16)
    flat_rows = normed.reshape(-1, D)
    query_rows = jnp.dot(flat_rows, query_matrix, preferred_element_type=jnp.float32).astype(jnp.bfloat16)
    query_rows = query_rows.reshape(N_EXPERT, SEQ, HEADS, HEAD_WIDTH)
    key_vectors = jnp.dot(flat_rows, key_matrix, preferred_element_type=jnp.float32).astype(jnp.bfloat16)
    key_vectors = key_vectors.reshape(N_EXPERT, SEQ, HEAD_WIDTH)
    value_vectors = jnp.dot(flat_rows, value_matrix, preferred_element_type=jnp.float32).astype(jnp.bfloat16)
    value_vectors = value_vectors.reshape(N_EXPERT, SEQ, HEAD_WIDTH)
    attention_scores = jnp.einsum('coal,cjl->caoj', query_rows.astype(jnp.float32), key_vectors.astype(jnp.float32)) * HEAD_WIDTH ** (-0.5)
    positions = jnp.arange(SEQ, dtype=jnp.int32)
    causal = positions[None, :] <= positions[:, None]
    attention_scores = jnp.where(causal[None, None], attention_scores, -1e+30)
    highest = lax.optimization_barrier(jnp.max(attention_scores, axis=-1, keepdims=True))
    exponent = jnp.exp(attention_scores - highest)
    attention_probabilities = (exponent / lax.optimization_barrier(jnp.sum(exponent, axis=-1, keepdims=True))).astype(jnp.bfloat16)
    attended_values = jnp.einsum('xmpo,xot->xpmt', attention_probabilities.astype(jnp.float32), value_vectors.astype(jnp.float32))
    attended_values = attended_values.astype(jnp.bfloat16).reshape(-1, HEADS * HEAD_WIDTH)
    return jnp.dot(attended_values, out_matrix, preferred_element_type=jnp.float32).reshape(N_EXPERT, SEQ, D)

def reference(tokens, attn_norm, moe_norm, query_weight, key_weight, value_weight, out_weight, gate_proj, up_proj, down_proj, routes, weights_code):
    current = tokens
    layer_outputs = []
    for layer_index in range(LAYERS):
        sequences = current.reshape(MICRO, N_EXPERT, TOK_DEV, D).transpose(1, 0, 2, 3).reshape(N_EXPERT, SEQ, D)
        attended = attention(sequences, attn_norm[layer_index], query_weight[layer_index], key_weight[layer_index], value_weight[layer_index], out_weight[layer_index])
        attended = attended.reshape(N_EXPERT, MICRO, TOK_DEV, D).transpose(1, 0, 2, 3).reshape(MICRO * TOKENS, D)
        flat_input = current.reshape(-1, D).astype(jnp.float32)
        normed = rms_scale(flat_input, moe_norm[layer_index]).astype(jnp.bfloat16)
        gate_all = gate_proj[layer_index]
        up_all = up_proj[layer_index]
        down_all = down_proj[layer_index]

        def micro_mixture(micro_item):
            return mixture(micro_item[0], micro_item[1], micro_item[2], gate_all, up_all, down_all)
        mixed = lax.map(micro_mixture, (normed.reshape(MICRO, TOKENS, D), routes[layer_index], weights_code[layer_index]))
        mixed = mixed.reshape(MICRO * TOKENS, D)
        current = (flat_input + attended + mixed).astype(jnp.bfloat16).reshape(MICRO, TOKENS, D)
        layer_outputs.append(current)
    return jnp.stack(layer_outputs)
```

```python
import jax
import jax.numpy as jnp
from jax import lax
from jax.sharding import PartitionSpec as P

epsilon = 1e-06


def shifted(value, axis, steps):
    count = lax.axis_size(axis)
    initial, last = (max(0, -steps), min(count, count - steps))
    return lax.ppermute(value, axis, [(source, source + steps) for source in range(initial, last)])


def rms_scale(features, gain_vector):
    return (
        features
        * lax.rsqrt(jnp.mean(features * features, axis=-1, keepdims=True) + epsilon)
        * gain_vector
    )


def expert_rows(slot_rows, gate_matrix, up_matrix, down_matrix):
    gated = jnp.dot(slot_rows, gate_matrix, preferred_element_type=jnp.float32)
    lifted = jnp.dot(slot_rows, up_matrix, preferred_element_type=jnp.float32)
    hidden = (jax.nn.silu(gated) * lifted).astype(jnp.bfloat16)
    return jnp.dot(hidden, down_matrix, preferred_element_type=jnp.float32).astype(jnp.bfloat16)


def route_tables(picks_block, codes_block, expert_count, capacity):
    tok_rows, pick_count = picks_block.shape
    flat_ids = picks_block.reshape(-1)
    matches = (flat_ids[:, None] == jnp.arange(expert_count, dtype=jnp.int32)[None, :]).astype(
        jnp.int32
    )
    slot_ranks = jnp.sum((jnp.cumsum(matches, axis=0) - matches) * matches, axis=1)
    columns = flat_ids * capacity + slot_ranks
    onehot = (
        columns[:, None] == jnp.arange(expert_count * capacity, dtype=jnp.int32)[None, :]
    ).astype(jnp.float32)
    onehot = onehot.reshape(tok_rows, pick_count, expert_count * capacity)
    scatter_table = jnp.sum(onehot, axis=1).astype(jnp.bfloat16)
    pick_weights = codes_block.astype(jnp.float32) / 64.0
    combine_table = jnp.sum(onehot * pick_weights[:, :, None], axis=1).astype(jnp.bfloat16)
    return (scatter_table, combine_table)


def shards(
    tokens,
    attn_norm,
    moe_norm,
    query_weight,
    key_weight,
    value_weight,
    out_weight,
    gate_proj,
    up_proj,
    down_proj,
    routes,
    weights_code,
):
    section_count = lax.axis_size("section")
    section_index = lax.axis_index("section")
    expert_devices = lax.axis_size("expert")
    micro_count, tok_rows, model_width = tokens.shape
    pick_count = routes.shape[3]
    expert_count = expert_devices * gate_proj.shape[1]
    capacity = min(tok_rows, tok_rows * pick_count * 4 // (3 * expert_count))
    head_size = key_weight.shape[-1]
    head_count = query_weight.shape[-1] // head_size
    full_mixed = lax.all_gather(
        jnp.concatenate([query_weight[0], key_weight[0], value_weight[0]], axis=-1),
        "expert",
        axis=0,
        tiled=True,
    )
    full_out = lax.all_gather(out_weight[0], "expert", axis=0, tiled=True)
    lag = 2 if section_count <= 2 else 1
    score_scale = head_size ** (-0.5)
    attn_gain = attn_norm[0]
    moe_gain = moe_norm[0]
    gate_matrix = gate_proj[0, 0]
    up_matrix = up_proj[0, 0]
    down_matrix = down_proj[0, 0]
    scatter_tables, combine_tables = jax.vmap(
        lambda picks, codes: route_tables(picks, codes, expert_count, capacity)
    )(routes[0], weights_code[0])

    def attend(wide_input, tick, keys, values):
        normed = rms_scale(wide_input, attn_gain).astype(jnp.bfloat16)
        projected = jnp.dot(normed, full_mixed, preferred_element_type=jnp.float32).astype(
            jnp.bfloat16
        )
        query_rows = projected[:, : head_count * head_size].reshape(
            tok_rows, head_count, head_size
        )
        keys.append(projected[:, head_count * head_size : (head_count + 1) * head_size])
        values.append(projected[:, (head_count + 1) * head_size :])
        oldest = max(0, tick + 1 - micro_count)
        key_vectors = jnp.concatenate(keys[oldest:], axis=0)
        value_vectors = jnp.concatenate(values[oldest:], axis=0)
        attention_scores = (
            jnp.einsum("qhd,kd->hqk", query_rows, key_vectors, preferred_element_type=jnp.float32)
            * score_scale
        )
        span = (tick + 1 - oldest) * tok_rows
        places = jnp.arange(span, dtype=jnp.int32)[None, :] + oldest * tok_rows
        query_places = tick * tok_rows + jnp.arange(tok_rows, dtype=jnp.int32)[:, None]
        causal = (places <= query_places) & (
            (places >= lag * section_index * tok_rows) | (places == query_places)
        )
        attention_scores = jnp.where(causal[None], attention_scores, -1e30)
        highest = jnp.max(attention_scores, axis=-1, keepdims=True)
        exponent = jnp.exp(attention_scores - highest)
        attention_probabilities = (exponent / jnp.sum(exponent, axis=-1, keepdims=True)).astype(
            jnp.bfloat16
        )
        attended_values = jnp.einsum(
            "hqk,kd->qhd",
            attention_probabilities,
            value_vectors,
            preferred_element_type=jnp.float32,
        )
        attended_values = attended_values.astype(jnp.bfloat16).reshape(
            tok_rows, head_count * head_size
        )
        return jnp.dot(attended_values, full_out, preferred_element_type=jnp.float32)

    def mixture(wide_input, scatter_table, combine_table):
        moe_input = rms_scale(wide_input, moe_gain).astype(jnp.bfloat16)
        outgoing = jnp.einsum(
            "te,td->ed", scatter_table, moe_input, preferred_element_type=jnp.float32
        )
        outgoing = outgoing.astype(jnp.bfloat16).reshape(expert_count, capacity, model_width)
        arrived = lax.all_to_all(outgoing, "expert", split_axis=0, concat_axis=0, tiled=True)
        produced = expert_rows(
            arrived.reshape(-1, model_width), gate_matrix, up_matrix, down_matrix
        ).reshape(arrived.shape)
        returned = lax.all_to_all(produced, "expert", split_axis=0, concat_axis=0, tiled=True)
        return jnp.dot(
            combine_table, returned.reshape(-1, model_width), preferred_element_type=jnp.float32
        )

    keys, values, results, inbound = [], [], [], []
    for tick in range(micro_count + lag * (section_count - 1)):
        clipped = jnp.clip(tick - lag * section_index, 0, micro_count - 1)
        layer_input = tokens[min(tick, micro_count - 1)]
        if tick >= lag:
            layer_input = jnp.where(section_index == 0, layer_input, inbound[tick - lag])
        wide_input = layer_input.astype(jnp.float32)
        mixed = mixture(
            wide_input,
            lax.dynamic_index_in_dim(scatter_tables, clipped, 0, keepdims=False),
            lax.dynamic_index_in_dim(combine_tables, clipped, 0, keepdims=False),
        )
        attended = attend(wide_input, tick, keys, values)
        results.append((wide_input + attended + mixed).astype(jnp.bfloat16))
        if tick + lag < micro_count + lag * (section_count - 1):
            inbound.append(shifted(results[-1], "section", 1))
    stacked = jnp.stack(results)
    return lax.dynamic_slice_in_dim(stacked, lag * section_index, micro_count, 0)[None]


def solution(mesh):
    placed = (
        P(None, "expert", None),
        P("section", None),
        P("section", None),
        P("section", "expert", None),
        P("section", "expert", None),
        P("section", "expert", None),
        P("section", "expert", None),
        P("section", "expert", None, None),
        P("section", "expert", None, None),
        P("section", "expert", None, None),
        P("section", None, "expert", None),
        P("section", None, "expert", None),
    )
    return jax.shard_map(
        shards,
        mesh=mesh,
        in_specs=placed,
        out_specs=P("section", None, "expert", None),
        check_vma=False,
    )
```

```python
import jax
import jax.numpy as jnp
from jax import lax
from jax.sharding import PartitionSpec as P

epsilon = 1e-06


def shifted(value, axis, steps):
    count = lax.axis_size(axis)
    initial, last = (max(0, -steps), min(count, count - steps))
    return lax.ppermute(value, axis, [(source, source + steps) for source in range(initial, last)])


def rms_scale(features, gain_vector):
    return (
        features
        * lax.rsqrt(jnp.mean(features * features, axis=-1, keepdims=True) + epsilon)
        * gain_vector
    )


def expert_rows(slot_rows, gate_matrix, up_matrix, down_matrix):
    gated = jnp.dot(slot_rows, gate_matrix, preferred_element_type=jnp.float32)
    lifted = jnp.dot(slot_rows, up_matrix, preferred_element_type=jnp.float32)
    hidden = (jax.nn.silu(gated) * lifted).astype(jnp.bfloat16)
    return jnp.dot(hidden, down_matrix, preferred_element_type=jnp.float32).astype(jnp.bfloat16)


def route_tables(picks_block, codes_block, expert_count, capacity, member, members):
    tok_rows, pick_count = picks_block.shape
    flat_ids = picks_block.reshape(-1)
    matches = (flat_ids[:, None] == jnp.arange(expert_count, dtype=jnp.int32)[None, :]).astype(
        jnp.int32
    )
    slot_ranks = jnp.sum((jnp.cumsum(matches, axis=0) - matches) * matches, axis=1)
    columns = (flat_ids * members + member) * capacity + slot_ranks
    capacity = members * capacity
    onehot = (
        columns[:, None] == jnp.arange(expert_count * capacity, dtype=jnp.int32)[None, :]
    ).astype(jnp.float32)
    onehot = onehot.reshape(tok_rows, pick_count, expert_count * capacity)
    scatter_table = jnp.sum(onehot, axis=1).astype(jnp.bfloat16)
    pick_weights = codes_block.astype(jnp.float32) / 64.0
    combine_table = jnp.sum(onehot * pick_weights[:, :, None], axis=1).astype(jnp.bfloat16)
    return (scatter_table, combine_table)


def shards(
    tokens,
    attn_norm,
    moe_norm,
    query_weight,
    key_weight,
    value_weight,
    out_weight,
    gate_proj,
    up_proj,
    down_proj,
    routes,
    weights_code,
):
    section_count = lax.axis_size("section")
    section_index = lax.axis_index("section")
    expert_devices = lax.axis_size("expert")
    micro_count, tok_rows, model_width = tokens.shape
    pick_count = routes.shape[3]
    expert_count = expert_devices * gate_proj.shape[1]
    capacity = min(tok_rows, tok_rows * pick_count * 4 // (3 * expert_count))
    head_size = key_weight.shape[-1]
    head_count = query_weight.shape[-1] // head_size
    full_mixed = lax.all_gather(
        jnp.concatenate([query_weight[0], key_weight[0], value_weight[0]], axis=-1),
        "expert",
        axis=0,
        tiled=True,
    )
    full_out = lax.all_gather(out_weight[0], "expert", axis=0, tiled=True)
    members = 2 if section_count <= 2 and micro_count % 2 == 0 else 1
    group_count, block_rows = micro_count // members, members * tok_rows
    lag = 1
    score_scale = head_size ** (-0.5)
    attn_gain = attn_norm[0]
    moe_gain = moe_norm[0]
    gate_matrix = gate_proj[0, 0]
    up_matrix = up_proj[0, 0]
    down_matrix = down_proj[0, 0]
    group_slots = members * capacity

    def member_tables(picks, codes, member):
        return route_tables(picks, codes, expert_count, capacity, member, members)

    scatter_tables, combine_tables = jax.vmap(member_tables)(
        routes[0], weights_code[0], jnp.arange(micro_count, dtype=jnp.int32) % members
    )
    scatter_tables = scatter_tables.reshape(group_count, block_rows, -1)
    combine_tables = combine_tables.reshape(group_count, block_rows, -1)
    token_groups = tokens.reshape(group_count, block_rows, model_width)

    def attend(wide_input, tick, keys, values):
        normed = rms_scale(wide_input, attn_gain).astype(jnp.bfloat16)
        projected = jnp.dot(normed, full_mixed, preferred_element_type=jnp.float32).astype(
            jnp.bfloat16
        )
        query_rows = projected[:, : head_count * head_size].reshape(
            block_rows, head_count, head_size
        )
        keys.append(projected[:, head_count * head_size : (head_count + 1) * head_size])
        values.append(projected[:, (head_count + 1) * head_size :])
        oldest = max(0, tick + 1 - group_count)
        key_vectors = jnp.concatenate(keys[oldest:], axis=0)
        value_vectors = jnp.concatenate(values[oldest:], axis=0)
        attention_scores = (
            jnp.einsum("qhd,kd->hqk", query_rows, key_vectors, preferred_element_type=jnp.float32)
            * score_scale
        )
        span = (tick + 1 - oldest) * block_rows
        places = jnp.arange(span, dtype=jnp.int32)[None, :] + oldest * block_rows
        query_places = tick * block_rows + jnp.arange(block_rows, dtype=jnp.int32)[:, None]
        causal = (places <= query_places) & (
            (places >= lag * section_index * block_rows) | (places == query_places)
        )
        attention_scores = jnp.where(causal[None], attention_scores, -1e30)
        highest = jnp.max(attention_scores, axis=-1, keepdims=True)
        exponent = jnp.exp(attention_scores - highest)
        attention_probabilities = (exponent / jnp.sum(exponent, axis=-1, keepdims=True)).astype(
            jnp.bfloat16
        )
        attended_values = jnp.einsum(
            "hqk,kd->qhd",
            attention_probabilities,
            value_vectors,
            preferred_element_type=jnp.float32,
        )
        attended_values = attended_values.astype(jnp.bfloat16).reshape(
            block_rows, head_count * head_size
        )
        return jnp.dot(attended_values, full_out, preferred_element_type=jnp.float32)

    def mixture(wide_input, scatter_table, combine_table):
        moe_input = rms_scale(wide_input, moe_gain).astype(jnp.bfloat16)
        outgoing = jnp.einsum(
            "te,td->ed", scatter_table, moe_input, preferred_element_type=jnp.float32
        )
        outgoing = outgoing.astype(jnp.bfloat16).reshape(expert_count, group_slots, model_width)
        arrived = lax.all_to_all(outgoing, "expert", split_axis=0, concat_axis=0, tiled=True)
        produced = expert_rows(
            arrived.reshape(-1, model_width), gate_matrix, up_matrix, down_matrix
        ).reshape(arrived.shape)
        returned = lax.all_to_all(produced, "expert", split_axis=0, concat_axis=0, tiled=True)
        return jnp.dot(
            combine_table, returned.reshape(-1, model_width), preferred_element_type=jnp.float32
        )

    keys, values, results, inbound = [], [], [], []
    for tick in range(group_count + lag * (section_count - 1)):
        clipped = jnp.clip(tick - lag * section_index, 0, group_count - 1)
        layer_input = token_groups[min(tick, group_count - 1)]
        if tick >= lag:
            layer_input = jnp.where(section_index == 0, layer_input, inbound[tick - lag])
        wide_input = layer_input.astype(jnp.float32)
        mixed = mixture(
            wide_input,
            lax.dynamic_index_in_dim(scatter_tables, clipped, 0, keepdims=False),
            lax.dynamic_index_in_dim(combine_tables, clipped, 0, keepdims=False),
        )
        attended = attend(wide_input, tick, keys, values)
        results.append((wide_input + attended + mixed).astype(jnp.bfloat16))
        if tick + lag < group_count + lag * (section_count - 1):
            inbound.append(shifted(results[-1], "section", 1))
    stacked = jnp.stack(results)
    chosen = lax.dynamic_slice_in_dim(stacked, lag * section_index, group_count, 0)
    return chosen.reshape(1, micro_count, tok_rows, model_width)


def solution(mesh):
    placed = (
        P(None, "expert", None),
        P("section", None),
        P("section", None),
        P("section", "expert", None),
        P("section", "expert", None),
        P("section", "expert", None),
        P("section", "expert", None),
        P("section", "expert", None, None),
        P("section", "expert", None, None),
        P("section", "expert", None, None),
        P("section", None, "expert", None),
        P("section", None, "expert", None),
    )
    return jax.shard_map(
        shards,
        mesh=mesh,
        in_specs=placed,
        out_specs=P("section", None, "expert", None),
        check_vma=False,
    )
```

```python
import functools

import jax
import jax.numpy as jnp
from jax import lax
from jax.experimental import pallas as pl
from jax.experimental.pallas import tpu as pltpu
from jax.sharding import PartitionSpec as P

epsilon = 1e-06


def shifted(value, axis, steps):
    count = lax.axis_size(axis)
    initial, last = (max(0, -steps), min(count, count - steps))
    return lax.ppermute(value, axis, [(source, source + steps) for source in range(initial, last)])


def rms_scale(features, gain_vector):
    return (
        features
        * lax.rsqrt(jnp.mean(features * features, axis=-1, keepdims=True) + epsilon)
        * gain_vector
    )


def expert_rows(slot_rows, gate_matrix, up_matrix, down_matrix):
    gated = jnp.dot(slot_rows, gate_matrix, preferred_element_type=jnp.float32)
    lifted = jnp.dot(slot_rows, up_matrix, preferred_element_type=jnp.float32)
    hidden = (jax.nn.silu(gated) * lifted).astype(jnp.bfloat16)
    return jnp.dot(hidden, down_matrix, preferred_element_type=jnp.float32).astype(jnp.bfloat16)


def route_tables(picks_block, codes_block, expert_count, capacity, member, members):
    tok_rows, pick_count = picks_block.shape
    flat_ids = picks_block.reshape(-1)
    matches = (flat_ids[:, None] == jnp.arange(expert_count, dtype=jnp.int32)[None, :]).astype(
        jnp.int32
    )
    slot_ranks = jnp.sum((jnp.cumsum(matches, axis=0) - matches) * matches, axis=1)
    columns = (flat_ids * members + member) * capacity + slot_ranks
    capacity = members * capacity
    onehot = (
        columns[:, None] == jnp.arange(expert_count * capacity, dtype=jnp.int32)[None, :]
    ).astype(jnp.float32)
    onehot = onehot.reshape(tok_rows, pick_count, expert_count * capacity)
    named_slots = jnp.sum(
        (matches * (slot_ranks + 1)[:, None]).reshape(tok_rows, pick_count, expert_count), axis=1
    ).astype(jnp.bfloat16)
    named_slots = jnp.pad(named_slots, ((0, 0), (0, -expert_count % 128)))
    pick_weights = codes_block.astype(jnp.float32) / 64.0
    combine_table = jnp.sum(onehot * pick_weights[:, :, None], axis=1).astype(jnp.bfloat16)
    return (named_slots, combine_table)


def gather_kernel(device_count, operand_count, *refs):
    sources, targets = refs[:operand_count], refs[operand_count : 2 * operand_count]
    own_sem, send_z, recv_z, send_y, recv_y, send_c, recv_c = refs[2 * operand_count :]
    me = lax.axis_index("expert")
    depth = device_count // 4
    place_c, place_y, place_z = lax.rem(me, 2), lax.rem(me // 2, 2), me // 4

    def index_of(z, y, c):
        return (z * 2 + y) * 2 + c

    partners = [index_of(lax.rem(place_z + k, depth), place_y, place_c) for k in range(1, depth)]
    origins = [
        index_of(lax.rem(place_z + depth - k, depth), place_y, place_c) for k in range(depth)
    ]
    crossed = [
        index_of(lax.rem(place_z + depth - k, depth), 1 - place_y, place_c) for k in range(depth)
    ]
    partner_y = index_of(place_z, 1 - place_y, place_c)
    partner_c = index_of(place_z, place_y, 1 - place_c)

    barrier = pltpu.get_barrier_semaphore()
    for peer in partners + [partner_y, partner_c]:
        pl.semaphore_signal(
            barrier, inc=1, device_id={"expert": peer}, device_id_type=pl.DeviceIdType.MESH
        )
    pl.semaphore_wait(barrier, depth + 1)

    def send(source, target, send_sem, recv_sem, peer):
        copy = pltpu.make_async_remote_copy(
            src_ref=source,
            dst_ref=target,
            send_sem=send_sem,
            recv_sem=recv_sem,
            device_id={"expert": peer},
            device_id_type=pl.DeviceIdType.MESH,
        )
        copy.start()
        return copy

    owned = []
    along_z = [[None] * depth for _ in range(operand_count)]
    along_y = [[None] * depth for _ in range(operand_count)]
    along_c = [[None] * (2 * depth) for _ in range(operand_count)]
    for a in range(operand_count):
        for k in range(1, depth):
            along_z[a][k] = send(
                sources[a],
                targets[a].at[me],
                send_z.at[a, k],
                recv_z.at[a, k],
                partners[k - 1],
            )
        along_y[a][0] = send(
            sources[a], targets[a].at[me], send_y.at[a, 0], recv_y.at[a, 0], partner_y
        )
        along_c[a][0] = send(
            sources[a], targets[a].at[me], send_c.at[a, 0], recv_c.at[a, 0], partner_c
        )
        owned.append(pltpu.make_async_copy(sources[a], targets[a].at[me], own_sem.at[a]))
        owned[a].start()
    for a in range(operand_count):
        for k in range(1, depth):
            along_z[a][k].wait_recv()
            block = targets[a].at[origins[k]]
            along_y[a][k] = send(block, block, send_y.at[a, k], recv_y.at[a, k], partner_y)
            along_c[a][k] = send(block, block, send_c.at[a, k], recv_c.at[a, k], partner_c)
    for a in range(operand_count):
        for k in range(depth):
            along_y[a][k].wait_recv()
            block = targets[a].at[crossed[k]]
            along_c[a][depth + k] = send(
                block, block, send_c.at[a, depth + k], recv_c.at[a, depth + k], partner_c
            )
    for a in range(operand_count):
        for k in range(2 * depth):
            along_c[a][k].wait_recv()
        for copy in along_z[a][1:] + along_y[a] + along_c[a]:
            copy.wait_send()
        owned[a].wait()


def gather_all(operands, collective_id):
    device_count, operand_count = lax.axis_size("expert"), len(operands)
    depth = device_count // 4
    pairs = pltpu.SemaphoreType.DMA((operand_count, depth))
    doubles = pltpu.SemaphoreType.DMA((operand_count, 2 * depth))
    return pl.pallas_call(
        functools.partial(gather_kernel, device_count, operand_count),
        out_shape=[
            jax.ShapeDtypeStruct((device_count,) + operand.shape, operand.dtype)
            for operand in operands
        ],
        in_specs=[pl.BlockSpec(memory_space=pltpu.VMEM)] * operand_count,
        out_specs=[pl.BlockSpec(memory_space=pl.ANY)] * operand_count,
        scratch_shapes=[
            pltpu.SemaphoreType.DMA((operand_count,)),
            pairs,
            pairs,
            pairs,
            pairs,
            doubles,
            doubles,
        ],
        compiler_params=pltpu.CompilerParams(collective_id=collective_id, has_side_effects=True),
    )(*operands)


def shards(
    tokens,
    attn_norm,
    moe_norm,
    query_weight,
    key_weight,
    value_weight,
    out_weight,
    gate_proj,
    up_proj,
    down_proj,
    routes,
    weights_code,
):
    section_count = lax.axis_size("section")
    section_index = lax.axis_index("section")
    expert_devices = lax.axis_size("expert")
    micro_count, tok_rows, model_width = tokens.shape
    pick_count = routes.shape[3]
    expert_count = expert_devices * gate_proj.shape[1]
    capacity = min(tok_rows, tok_rows * pick_count * 4 // (3 * expert_count))
    head_size = key_weight.shape[-1]
    head_count = query_weight.shape[-1] // head_size
    mixed_blocks, out_blocks = gather_all(
        [
            jnp.concatenate([query_weight[0], key_weight[0], value_weight[0]], axis=-1),
            out_weight[0],
        ],
        0,
    )
    full_mixed = mixed_blocks.reshape(model_width, -1)
    full_out = out_blocks.reshape(-1, model_width)
    members = 2 if section_count <= 2 and micro_count % 2 == 0 else 1
    group_count, block_rows = micro_count // members, members * tok_rows
    lag = 1
    score_scale = head_size ** (-0.5)
    attn_gain = attn_norm[0]
    moe_gain = moe_norm[0]
    gate_matrix = gate_proj[0, 0]
    up_matrix = up_proj[0, 0]
    down_matrix = down_proj[0, 0]
    group_slots = members * capacity

    def member_tables(picks, codes, member):
        return route_tables(picks, codes, expert_count, capacity, member, members)

    slot_tables, combine_tables = jax.vmap(member_tables)(
        routes[0], weights_code[0], jnp.arange(micro_count, dtype=jnp.int32) % members
    )
    slot_tables = slot_tables.reshape(group_count, block_rows, -1)
    combine_tables = combine_tables.reshape(group_count, block_rows, -1)
    token_groups = tokens.reshape(group_count, block_rows, model_width)

    def attend(wide_input, tick, keys, values):
        normed = rms_scale(wide_input, attn_gain).astype(jnp.bfloat16)
        projected = jnp.dot(normed, full_mixed, preferred_element_type=jnp.float32).astype(
            jnp.bfloat16
        )
        query_rows = projected[:, : head_count * head_size].reshape(
            block_rows, head_count, head_size
        )
        keys.append(projected[:, head_count * head_size : (head_count + 1) * head_size])
        values.append(projected[:, (head_count + 1) * head_size :])
        oldest = max(0, tick + 1 - group_count)
        key_vectors = jnp.concatenate(keys[oldest:], axis=0)
        value_vectors = jnp.concatenate(values[oldest:], axis=0)
        attention_scores = (
            jnp.einsum("qhd,kd->hqk", query_rows, key_vectors, preferred_element_type=jnp.float32)
            * score_scale
        )
        span = (tick + 1 - oldest) * block_rows
        places = jnp.arange(span, dtype=jnp.int32)[None, :] + oldest * block_rows
        query_places = tick * block_rows + jnp.arange(block_rows, dtype=jnp.int32)[:, None]
        causal = (places <= query_places) & (
            (places >= lag * section_index * block_rows) | (places == query_places)
        )
        attention_scores = jnp.where(causal[None], attention_scores, -1e30)
        highest = jnp.max(attention_scores, axis=-1, keepdims=True)
        exponent = jnp.exp(attention_scores - highest)
        attention_probabilities = (exponent / jnp.sum(exponent, axis=-1, keepdims=True)).astype(
            jnp.bfloat16
        )
        attended_values = jnp.einsum(
            "hqk,kd->qhd",
            attention_probabilities,
            value_vectors,
            preferred_element_type=jnp.float32,
        )
        attended_values = attended_values.astype(jnp.bfloat16).reshape(
            block_rows, head_count * head_size
        )
        return jnp.dot(attended_values, full_out, preferred_element_type=jnp.float32)

    def mixture(wide_input, slot_table, combine_table):
        moe_input = rms_scale(wide_input, moe_gain).astype(jnp.bfloat16)
        (gathered,) = gather_all([jnp.concatenate([moe_input, slot_table], axis=-1)], 1)
        named = lax.dynamic_slice_in_dim(
            gathered, model_width + lax.axis_index("expert"), 1, axis=2
        ).reshape(expert_devices, members, 1, tok_rows)
        slots = jnp.arange(1, capacity + 1, dtype=jnp.int32).astype(jnp.bfloat16)
        chosen = (named == slots[None, None, :, None]).astype(jnp.bfloat16)
        source_rows = gathered[:, :, :model_width].reshape(
            expert_devices, members, tok_rows, model_width
        )
        arrived = jnp.einsum(
            "nmsi,nmid->nmsd", chosen, source_rows, preferred_element_type=jnp.float32
        )
        arrived = arrived.astype(jnp.bfloat16).reshape(expert_count, group_slots, model_width)
        produced = expert_rows(
            arrived.reshape(-1, model_width), gate_matrix, up_matrix, down_matrix
        ).reshape(arrived.shape)
        returned = lax.all_to_all(produced, "expert", split_axis=0, concat_axis=0, tiled=True)
        return jnp.dot(
            combine_table, returned.reshape(-1, model_width), preferred_element_type=jnp.float32
        )

    keys, values, results, inbound = [], [], [], []
    for tick in range(group_count + lag * (section_count - 1)):
        clipped = jnp.clip(tick - lag * section_index, 0, group_count - 1)
        layer_input = token_groups[min(tick, group_count - 1)]
        if tick >= lag:
            layer_input = jnp.where(section_index == 0, layer_input, inbound[tick - lag])
        wide_input = layer_input.astype(jnp.float32)
        mixed = mixture(
            wide_input,
            lax.dynamic_index_in_dim(slot_tables, clipped, 0, keepdims=False),
            lax.dynamic_index_in_dim(combine_tables, clipped, 0, keepdims=False),
        )
        attended = attend(wide_input, tick, keys, values)
        results.append((wide_input + attended + mixed).astype(jnp.bfloat16))
        if tick + lag < group_count + lag * (section_count - 1):
            inbound.append(shifted(results[-1], "section", 1))
    stacked = jnp.stack(results)
    chosen = lax.dynamic_slice_in_dim(stacked, lag * section_index, group_count, 0)
    return chosen.reshape(1, micro_count, tok_rows, model_width)


def solution(mesh):
    placed = (
        P(None, "expert", None),
        P("section", None),
        P("section", None),
        P("section", "expert", None),
        P("section", "expert", None),
        P("section", "expert", None),
        P("section", "expert", None),
        P("section", "expert", None, None),
        P("section", "expert", None, None),
        P("section", "expert", None, None),
        P("section", None, "expert", None),
        P("section", None, "expert", None),
    )
    return jax.shard_map(
        shards,
        mesh=mesh,
        in_specs=placed,
        out_specs=P("section", None, "expert", None),
        check_vma=False,
    )
```

```python
import functools

import jax
import jax.numpy as jnp
from jax import lax
from jax.experimental import pallas as pl
from jax.experimental.pallas import tpu as pltpu
from jax.sharding import PartitionSpec as P

epsilon = 1e-06


def shifted(value, axis, steps):
    count = lax.axis_size(axis)
    initial, last = (max(0, -steps), min(count, count - steps))
    return lax.ppermute(value, axis, [(source, source + steps) for source in range(initial, last)])


def rms_scale(features, gain_vector):
    return (
        features
        * lax.rsqrt(jnp.mean(features * features, axis=-1, keepdims=True) + epsilon)
        * gain_vector
    )


def expert_rows(slot_rows, gate_matrix, up_matrix, down_matrix):
    gated = jnp.dot(slot_rows, gate_matrix, preferred_element_type=jnp.float32)
    lifted = jnp.dot(slot_rows, up_matrix, preferred_element_type=jnp.float32)
    hidden = (jax.nn.silu(gated) * lifted).astype(jnp.bfloat16)
    return jnp.dot(hidden, down_matrix, preferred_element_type=jnp.float32).astype(jnp.bfloat16)


def route_tables(picks_block, codes_block, expert_count, capacity, member, members):
    tok_rows, pick_count = picks_block.shape
    flat_ids = picks_block.reshape(-1)
    matches = (flat_ids[:, None] == jnp.arange(expert_count, dtype=jnp.int32)[None, :]).astype(
        jnp.int32
    )
    slot_ranks = jnp.sum((jnp.cumsum(matches, axis=0) - matches) * matches, axis=1)
    columns = (flat_ids * members + member) * capacity + slot_ranks
    capacity = members * capacity
    onehot = (
        columns[:, None] == jnp.arange(expert_count * capacity, dtype=jnp.int32)[None, :]
    ).astype(jnp.float32)
    onehot = onehot.reshape(tok_rows, pick_count, expert_count * capacity)
    named_slots = jnp.sum(
        (matches * (slot_ranks + 1)[:, None]).reshape(tok_rows, pick_count, expert_count), axis=1
    ).astype(jnp.bfloat16)
    named_slots = jnp.pad(named_slots, ((0, 0), (0, -expert_count % 128)))
    pick_weights = codes_block.astype(jnp.float32) / 64.0
    combine_table = jnp.sum(onehot * pick_weights[:, :, None], axis=1).astype(jnp.bfloat16)
    return (named_slots, combine_table)


def gather_kernel(device_count, operand_count, *refs):
    sources, targets = refs[:operand_count], refs[operand_count : 2 * operand_count]
    own_sem, send_up, send_down, recv_z, send_y, recv_y, send_c, recv_c = refs[2 * operand_count :]
    me = lax.axis_index("expert")
    depth = device_count // 4
    place_c, place_y, place_z = lax.rem(me, 2), lax.rem(me // 2, 2), me // 4

    def index_of(z, y, c):
        return (z * 2 + y) * 2 + c

    upper, lower = index_of(place_z + 1, place_y, place_c), index_of(place_z - 1, place_y, place_c)
    partner_y = index_of(place_z, 1 - place_y, place_c)
    partner_c = index_of(place_z, place_y, 1 - place_c)
    has_upper, has_lower = place_z < depth - 1, place_z > 0
    operands = range(operand_count)
    barrier = pltpu.get_barrier_semaphore()

    def greet(peer):
        pl.semaphore_signal(
            barrier, inc=1, device_id={"expert": peer}, device_id_type=pl.DeviceIdType.MESH
        )

    for step in (1, depth - 1):
        greet(index_of(lax.rem(place_z + step, depth), place_y, place_c))
    greet(partner_y)
    greet(partner_c)
    pl.semaphore_wait(barrier, 4)

    def transfer(source, target, send_sem, recv_sem, peer):
        return pltpu.make_async_remote_copy(
            src_ref=source,
            dst_ref=target,
            send_sem=send_sem,
            recv_sem=recv_sem,
            device_id={"expert": peer},
            device_id_type=pl.DeviceIdType.MESH,
        )

    def up(a, origin, source, target):
        return transfer(source, target, send_up.at[a, origin], recv_z.at[a, origin], upper)

    def down(a, origin, source, target):
        return transfer(source, target, send_down.at[a, origin], recv_z.at[a, origin], lower)

    def across(a, origin, source, target):
        return transfer(source, target, send_y.at[a, origin], recv_y.at[a, origin], partner_y)

    def beside(a, slot, source, target):
        return transfer(source, target, send_c.at[a, slot], recv_c.at[a, slot], partner_c)

    def own_block(a):
        source, target = sources[a], targets[a].at[me]
        pl.when(has_upper)(lambda: up(a, place_z, source, target).start())
        pl.when(has_lower)(lambda: down(a, place_z, source, target).start())
        across(a, place_z, source, target).start()
        beside(a, place_z, source, target).start()
        pltpu.make_async_copy(source, target, own_sem.at[a]).start()

    def relay(a, origin, onward, has_next):
        block = targets[a].at[index_of(origin, place_y, place_c)]
        onward(a, origin, block, block).wait_recv()
        pl.when(has_next)(lambda: onward(a, origin, block, block).start())
        across(a, origin, block, block).start()
        beside(a, origin, block, block).start()

    def crossed(a, origin):
        block = targets[a].at[index_of(origin, 1 - place_y, place_c)]
        across(a, origin, block, block).wait_recv()
        beside(a, depth + origin, block, block).start()

    for a in operands:
        own_block(a)
    for k in range(1, depth):
        for a in operands:
            pl.when(place_z >= k)(lambda: relay(a, place_z - k, up, has_upper))
            pl.when(place_z + k < depth)(lambda: relay(a, place_z + k, down, has_lower))
            if k == 1:
                crossed(a, place_z)
            else:
                pl.when(place_z >= k - 1)(lambda: crossed(a, place_z - (k - 1)))
                pl.when(place_z + k - 1 < depth)(lambda: crossed(a, place_z + (k - 1)))
    for a in operands:
        pl.when(place_z >= depth - 1)(lambda: crossed(a, place_z - (depth - 1)))
        pl.when(place_z + depth - 1 < depth)(lambda: crossed(a, place_z + (depth - 1)))
    for a in operands:
        block = sources[a]
        for slot in range(2 * depth):
            beside(a, slot, block, targets[a].at[me]).wait_recv()
            beside(a, slot, block, targets[a].at[me]).wait_send()
        for origin in range(depth):
            across(a, origin, block, targets[a].at[me]).wait_send()
            pl.when(has_upper & (place_z >= origin))(
                lambda: up(a, origin, block, targets[a].at[me]).wait_send()
            )
            pl.when(has_lower & (place_z <= origin))(
                lambda: down(a, origin, block, targets[a].at[me]).wait_send()
            )
        pltpu.make_async_copy(block, targets[a].at[me], own_sem.at[a]).wait()


def gather_all(operands, collective_id):
    device_count, operand_count = lax.axis_size("expert"), len(operands)
    depth = device_count // 4
    pairs = pltpu.SemaphoreType.DMA((operand_count, depth))
    doubles = pltpu.SemaphoreType.DMA((operand_count, 2 * depth))
    return pl.pallas_call(
        functools.partial(gather_kernel, device_count, operand_count),
        out_shape=[
            jax.ShapeDtypeStruct((device_count,) + operand.shape, operand.dtype)
            for operand in operands
        ],
        in_specs=[pl.BlockSpec(memory_space=pltpu.VMEM)] * operand_count,
        out_specs=[pl.BlockSpec(memory_space=pl.ANY)] * operand_count,
        scratch_shapes=[
            pltpu.SemaphoreType.DMA((operand_count,)),
            pairs,
            pairs,
            pairs,
            pairs,
            pairs,
            doubles,
            doubles,
        ],
        compiler_params=pltpu.CompilerParams(collective_id=collective_id, has_side_effects=True),
    )(*operands)


def shards(
    tokens,
    attn_norm,
    moe_norm,
    query_weight,
    key_weight,
    value_weight,
    out_weight,
    gate_proj,
    up_proj,
    down_proj,
    routes,
    weights_code,
):
    section_count = lax.axis_size("section")
    section_index = lax.axis_index("section")
    expert_devices = lax.axis_size("expert")
    micro_count, tok_rows, model_width = tokens.shape
    pick_count = routes.shape[3]
    expert_count = expert_devices * gate_proj.shape[1]
    capacity = min(tok_rows, tok_rows * pick_count * 4 // (3 * expert_count))
    head_size = key_weight.shape[-1]
    head_count = query_weight.shape[-1] // head_size
    mixed_blocks, out_blocks = gather_all(
        [
            jnp.concatenate([query_weight[0], key_weight[0], value_weight[0]], axis=-1),
            out_weight[0],
        ],
        0,
    )
    full_mixed = mixed_blocks.reshape(model_width, -1)
    full_out = out_blocks.reshape(-1, model_width)
    members = 2 if section_count <= 2 and micro_count % 2 == 0 else 1
    group_count, block_rows = micro_count // members, members * tok_rows
    lag = 1
    score_scale = head_size ** (-0.5)
    attn_gain = attn_norm[0]
    moe_gain = moe_norm[0]
    gate_matrix = gate_proj[0, 0]
    up_matrix = up_proj[0, 0]
    down_matrix = down_proj[0, 0]
    group_slots = members * capacity

    def member_tables(picks, codes, member):
        return route_tables(picks, codes, expert_count, capacity, member, members)

    slot_tables, combine_tables = jax.vmap(member_tables)(
        routes[0], weights_code[0], jnp.arange(micro_count, dtype=jnp.int32) % members
    )
    slot_tables = slot_tables.reshape(group_count, block_rows, -1)
    combine_tables = combine_tables.reshape(group_count, block_rows, -1)
    token_groups = tokens.reshape(group_count, block_rows, model_width)

    def attend(wide_input, tick, keys, values):
        normed = rms_scale(wide_input, attn_gain).astype(jnp.bfloat16)
        projected = jnp.dot(normed, full_mixed, preferred_element_type=jnp.float32).astype(
            jnp.bfloat16
        )
        query_rows = projected[:, : head_count * head_size].reshape(
            block_rows, head_count, head_size
        )
        keys.append(projected[:, head_count * head_size : (head_count + 1) * head_size])
        values.append(projected[:, (head_count + 1) * head_size :])
        oldest = max(0, tick + 1 - group_count)
        key_vectors = jnp.concatenate(keys[oldest:], axis=0)
        value_vectors = jnp.concatenate(values[oldest:], axis=0)
        attention_scores = (
            jnp.einsum("qhd,kd->hqk", query_rows, key_vectors, preferred_element_type=jnp.float32)
            * score_scale
        )
        span = (tick + 1 - oldest) * block_rows
        places = jnp.arange(span, dtype=jnp.int32)[None, :] + oldest * block_rows
        query_places = tick * block_rows + jnp.arange(block_rows, dtype=jnp.int32)[:, None]
        causal = (places <= query_places) & (
            (places >= lag * section_index * block_rows) | (places == query_places)
        )
        attention_scores = jnp.where(causal[None], attention_scores, -1e30)
        highest = jnp.max(attention_scores, axis=-1, keepdims=True)
        exponent = jnp.exp(attention_scores - highest)
        attention_probabilities = (exponent / jnp.sum(exponent, axis=-1, keepdims=True)).astype(
            jnp.bfloat16
        )
        attended_values = jnp.einsum(
            "hqk,kd->qhd",
            attention_probabilities,
            value_vectors,
            preferred_element_type=jnp.float32,
        )
        attended_values = attended_values.astype(jnp.bfloat16).reshape(
            block_rows, head_count * head_size
        )
        return jnp.dot(attended_values, full_out, preferred_element_type=jnp.float32)

    def mixture(wide_input, slot_table, combine_table):
        moe_input = rms_scale(wide_input, moe_gain).astype(jnp.bfloat16)
        gathered, named = gather_all([moe_input, slot_table], 1)
        named = lax.dynamic_slice_in_dim(named, lax.axis_index("expert"), 1, axis=2).reshape(
            expert_devices, members, 1, tok_rows
        )
        slots = jnp.arange(1, capacity + 1, dtype=jnp.int32).astype(jnp.bfloat16)
        chosen = (named == slots[None, None, :, None]).astype(jnp.bfloat16)
        source_rows = gathered.reshape(
            expert_devices, members, tok_rows, model_width
        )
        arrived = jnp.einsum(
            "nmsi,nmid->nmsd", chosen, source_rows, preferred_element_type=jnp.float32
        )
        arrived = arrived.astype(jnp.bfloat16).reshape(expert_count, group_slots, model_width)
        produced = expert_rows(
            arrived.reshape(-1, model_width), gate_matrix, up_matrix, down_matrix
        ).reshape(arrived.shape)
        returned = lax.all_to_all(produced, "expert", split_axis=0, concat_axis=0, tiled=True)
        return jnp.dot(
            combine_table, returned.reshape(-1, model_width), preferred_element_type=jnp.float32
        )

    keys, values, results, inbound = [], [], [], []
    for tick in range(group_count + lag * (section_count - 1)):
        clipped = jnp.clip(tick - lag * section_index, 0, group_count - 1)
        layer_input = token_groups[min(tick, group_count - 1)]
        if tick >= lag:
            layer_input = jnp.where(section_index == 0, layer_input, inbound[tick - lag])
        wide_input = layer_input.astype(jnp.float32)
        mixed = mixture(
            wide_input,
            lax.dynamic_index_in_dim(slot_tables, clipped, 0, keepdims=False),
            lax.dynamic_index_in_dim(combine_tables, clipped, 0, keepdims=False),
        )
        attended = attend(wide_input, tick, keys, values)
        results.append((wide_input + attended + mixed).astype(jnp.bfloat16))
        if tick + lag < group_count + lag * (section_count - 1):
            inbound.append(shifted(results[-1], "section", 1))
    stacked = jnp.stack(results)
    chosen = lax.dynamic_slice_in_dim(stacked, lag * section_index, group_count, 0)
    return chosen.reshape(1, micro_count, tok_rows, model_width)


def solution(mesh):
    placed = (
        P(None, "expert", None),
        P("section", None),
        P("section", None),
        P("section", "expert", None),
        P("section", "expert", None),
        P("section", "expert", None),
        P("section", "expert", None),
        P("section", "expert", None, None),
        P("section", "expert", None, None),
        P("section", "expert", None, None),
        P("section", None, "expert", None),
        P("section", None, "expert", None),
    )
    return jax.shard_map(
        shards,
        mesh=mesh,
        in_specs=placed,
        out_specs=P("section", None, "expert", None),
        check_vma=False,
    )
```
